32 devices in a mesh: groups: 2 (over y), frame: 4 (over z), quarter: 2 (over x), sub: 2 (over core).
Axes of the slice: x: 2, y: 2, z: 4, core: 2. Of those that a mesh axis runs over, the one named last changes fastest.
Arguments:
- queries: bfloat16 [16, 1024, 256], P(('groups', 'frame'), ('quarter', 'sub')), parts along dimension 0, may hold values from -36 to 36
- keys: bfloat16 [16, 1024, 256], P(('groups', 'frame'), ('quarter', 'sub')), parts along dimension 0, may hold values from -6 to 6
- values: bfloat16 [16, 1024, 256], P(('groups', 'frame'), ('quarter', 'sub')), parts along dimension 0, may hold values from -6 to 6
Outputs:
- attended: bfloat16 [16, 1024, 256], P(('groups', 'frame'), ('quarter', 'sub')), parts along dimension 0
The draws below stay inside these ranges and needn't reach their ends.
There are 2 independent parts, one for each index of `groups`. The reference program is written for one: setup_inputs(seed, part) draws one part's arguments, and reference() takes and returns one part's arrays. A program takes and returns all parts, laid end to end along the dimension named above; each array names one. Nothing has to cross between parts.
All inputs are finite; a program needn't handle non-finite values.
Results may differ from the reference program's by a relative error of at most 0.0028.
Values may be sent and summed in bfloat16 or wider, within the bound.
A program may use at most 64 MiB of HBM per device.

```python
import math
import jax
import jax.numpy as jnp
from jax import lax

HEAD_DIM = 128
STRIP = 16
FRAMES = 8
POS = 1024


def draw_keys(key, part):
    shape = (FRAMES, POS, 2 * HEAD_DIM)
    result = jnp.clip(jax.random.normal(jax.random.fold_in(key, 1), shape, jnp.float32), -6.0, 6.0)
    return result.astype(jnp.bfloat16)


def draw_queries(key, part):
    shape = (FRAMES, POS, 2 * HEAD_DIM)
    result = jnp.clip(3.0 * jax.random.normal(jax.random.fold_in(key, 201), shape, jnp.float32), -18.0, 18.0)
    return result.astype(jnp.bfloat16)


def block_scale(stream_key, shape, split, smallest, high):
    def one(axis_at, shards_of):
        steps = jax.random.uniform(jax.random.fold_in(jax.random.fold_in(stream_key, 6), axis_at), (shards_of,), jnp.float32, smallest / len(split), high / len(split))
        return jnp.repeat(jnp.exp(steps), shape[axis_at] // shards_of).reshape((-1,) + (1,) * (len(shape) - axis_at - 1))

    loudness = one(*split[0])
    for cut in split[1:]:
        loudness = loudness * one(*cut)
    return loudness


def normal_values(stream_key, extent, spread, reach, cuts=(), dtype=jnp.bfloat16):
    values = jax.random.normal(stream_key, extent, jnp.float32) * spread
    if len(cuts) > 0:
        values = block_scale(stream_key, extent, cuts, -0.22, 0.18) * values
    return jnp.clip(values, min=-reach, max=reach).astype(dtype)


def setup_inputs(seed: int = 0, part: int = 0) -> dict:
    seeds = jax.random.split(jax.random.key(seed), 4)
    part_keys = jax.random.split(jax.random.fold_in(seeds[3], part), 4)
    queries = draw_queries(jax.random.fold_in(jax.random.fold_in(seeds[3], part), 71), part)
    keys = draw_keys(jax.random.fold_in(jax.random.fold_in(seeds[3], part), 71), part)
    values = normal_values(part_keys[2], (FRAMES, POS, 2 * HEAD_DIM), 1.0, 6.0, ((0, 4), (1, 4)))
    return {"queries": queries, "keys": keys, "values": values}


def attend(query_rows, key_rows, value_rows):
    width = query_rows.shape[-1]
    scores = jnp.dot(query_rows, key_rows.T, preferred_element_type=jnp.float32) * (1.0 / math.sqrt(width))
    highest = lax.optimization_barrier(jnp.max(scores, axis=-1, keepdims=True))
    expo = jnp.exp(scores - highest)
    totals = lax.optimization_barrier(jnp.sum(expo, axis=-1, keepdims=True))
    mixed = jnp.dot(expo.astype(jnp.bfloat16), value_rows, preferred_element_type=jnp.float32)
    return (mixed / totals).astype(jnp.bfloat16)

def reference(queries, keys, values):
    block_rows = math.gcd(POS, 1024)
    block_count = POS // block_rows

    def spatial_frame(frame_data):
        query_frame, key_frame, value_frame = frame_data
        grouped = query_frame.reshape(block_count, block_rows, HEAD_DIM)
        mixed = lax.map(lambda block: attend(block, key_frame, value_frame), grouped)
        return mixed.reshape(POS, HEAD_DIM)
    spatial = lax.map(spatial_frame, (queries[..., :HEAD_DIM], keys[..., :HEAD_DIM], values[..., :HEAD_DIM]))
    strips_total = POS // STRIP

    def to_strips(array):
        part_two = array[..., HEAD_DIM:].reshape(FRAMES, strips_total, STRIP, HEAD_DIM)
        return part_two.transpose(1, 0, 2, 3).reshape(strips_total, FRAMES * STRIP, HEAD_DIM)

    def strip_attend(strip_data):
        return attend(strip_data[0], strip_data[1], strip_data[2])
    temporal = lax.map(strip_attend, (to_strips(queries), to_strips(keys), to_strips(values)))
    temporal = temporal.reshape(strips_total, FRAMES, STRIP, HEAD_DIM).transpose(1, 0, 2, 3).reshape(FRAMES, POS, HEAD_DIM)
    return jnp.concatenate([spatial, temporal], axis=-1)
```

```python
import functools
import math

import jax
import jax.numpy as jnp
from jax import lax
from jax.experimental import pallas as pl
from jax.experimental.pallas import tpu as pltpu
from jax.sharding import PartitionSpec as P

STRIP = 16
MESH = pl.DeviceIdType.MESH


def attend(query_rows, key_rows, value_rows, score_scale):
    scores = lax.dot_general(
        query_rows, key_rows, (((1,), (1,)), ((), ())), preferred_element_type=jnp.float32
    )
    highest = jnp.max(scores, axis=-1, keepdims=True)
    expo = jnp.exp((scores - highest) * score_scale)
    totals = jnp.sum(expo, axis=-1, keepdims=True)
    mixed = jnp.dot(expo.astype(jnp.bfloat16), value_rows, preferred_element_type=jnp.float32)
    return (mixed / totals).astype(jnp.bfloat16)


def kernel(
    sizes,
    q_in, k_in, v_in, out,
    q_sp, k_sp, v_sp, q_tm, k_tm, v_tm, o_tm, o_sp,
    local_sem, z_send, z_recv, r_send, r_recv, x_send, x_recv, s_send, s_recv,
):
    n, nq, ns, frames, tokens, width, chunks = sizes
    rows = tokens // n
    rows_chunk = rows // chunks
    score_scale = 1.0 / math.sqrt(width)
    me = lax.axis_index("frame")
    my_quarter = lax.axis_index("quarter")
    my_sub = lax.axis_index("sub")
    temporal_in = (q_in, k_in, v_in)
    temporal_buf = (q_tm, k_tm, v_tm)
    spatial_in = (k_in, v_in)
    spatial_buf = (k_sp, v_sp)
    first = slice(0, width)
    second = slice(width, 2 * width)

    barrier = pltpu.get_barrier_semaphore()
    for step in range(1, n):
        pl.semaphore_signal(
            barrier, inc=1, device_id={"frame": lax.rem(me + step, n)}, device_id_type=MESH
        )
    for step in range(1, nq):
        pl.semaphore_signal(
            barrier, inc=1, device_id={"quarter": lax.rem(my_quarter + step, nq)}, device_id_type=MESH
        )
    for step in range(1, ns):
        pl.semaphore_signal(
            barrier, inc=1, device_id={"sub": lax.rem(my_sub + step, ns)}, device_id_type=MESH
        )

    my_slot = my_quarter * ns + my_sub
    my_rows = pl.ds(pl.multiple_of(me * rows, STRIP), rows)
    my_tokens = pl.ds(pl.multiple_of(my_slot * tokens, tokens), tokens)
    my_frames = pl.ds(me * frames, frames)
    loads = [pltpu.make_async_copy(q_in.at[:, :, first], q_sp, local_sem.at[0])]
    for index in range(2):
        loads.append(
            pltpu.make_async_copy(
                spatial_in[index].at[:, :, first],
                spatial_buf[index].at[:, my_tokens, :],
                local_sem.at[1 + index],
            )
        )
    for index in range(3):
        loads.append(
            pltpu.make_async_copy(
                temporal_in[index].at[:, my_rows, second],
                temporal_buf[index].at[my_frames],
                local_sem.at[3 + index],
            )
        )
    for load in loads:
        load.start()

    pl.semaphore_wait(barrier, (n - 1) + (nq - 1) + (ns - 1))

    low = (me < n // 2).astype(jnp.int32)

    def peer_at(place):
        down = n - 1 - place
        down = down - (down <= me).astype(jnp.int32)
        up = place + (place >= me).astype(jnp.int32)
        return low * down + (1 - low) * up

    def strip_copy(index, chunk, place, target, source):
        lower = pl.multiple_of(target * rows + chunk * rows_chunk, STRIP)
        return pltpu.make_async_remote_copy(
            src_ref=temporal_in[index].at[:, pl.ds(lower, rows_chunk), second],
            dst_ref=temporal_buf[index].at[
                pl.ds(source * frames, frames), pl.ds(chunk * rows_chunk, rows_chunk), :
            ],
            send_sem=z_send.at[(index * chunks + chunk) * n + place],
            recv_sem=z_recv.at[(index * chunks + chunk) * n + source],
            device_id={"frame": target},
            device_id_type=MESH,
        )

    def return_copy(chunk, place, target, source):
        lower = pl.multiple_of(source * rows + chunk * rows_chunk, STRIP)
        return pltpu.make_async_remote_copy(
            src_ref=o_tm.at[
                pl.ds(target * frames, frames), pl.ds(chunk * rows_chunk, rows_chunk), :
            ],
            dst_ref=out.at[:, pl.ds(lower, rows_chunk), second],
            send_sem=r_send.at[chunk * n + place],
            recv_sem=r_recv.at[chunk * n + source],
            device_id={"frame": target},
            device_id_type=MESH,
        )

    def quarter_copy(index, frame, step, target, source):
        place = pl.ds(pl.multiple_of((source * ns + my_sub) * tokens, tokens), tokens)
        return pltpu.make_async_remote_copy(
            src_ref=spatial_in[index].at[frame, :, first],
            dst_ref=spatial_buf[index].at[frame, place, :],
            send_sem=x_send.at[(index * frames + frame) * nq + step],
            recv_sem=x_recv.at[(index * frames + frame) * nq + source],
            device_id={"quarter": target},
            device_id_type=MESH,
        )

    def sub_copy(index, frame, step, quarter_step, target, quarter, source):
        place = pl.ds(pl.multiple_of((quarter * ns + source) * tokens, tokens), tokens)
        landed = spatial_buf[index].at[frame, place, :]
        return pltpu.make_async_remote_copy(
            src_ref=spatial_in[index].at[frame, :, first] if quarter_step == 0 else landed,
            dst_ref=landed,
            send_sem=s_send.at[((index * frames + frame) * nq + quarter_step) * ns + step],
            recv_sem=s_recv.at[((index * frames + frame) * nq + quarter) * ns + source],
            device_id={"sub": target},
            device_id_type=MESH,
        )

    sent = []
    for chunk in range(chunks):
        for place in range(n - 1):
            for index in range(3):
                sent.append(strip_copy(index, chunk, place, peer_at(place), me))
                sent[-1].start()
        if chunk == 0:
            for frame in range(frames):
                for index in range(2):
                    for step in range(1, nq):
                        sent.append(
                            quarter_copy(
                                index, frame, step, lax.rem(my_quarter + step, nq), my_quarter
                            )
                        )
                        sent[-1].start()
                    for step in range(1, ns):
                        sent.append(
                            sub_copy(
                                index, frame, step, 0, lax.rem(my_sub + step, ns), my_quarter, my_sub
                            )
                        )
                        sent[-1].start()
    for load in loads:
        load.wait()

    def forward(frame):
        for step in range(1, nq):
            source = lax.rem(my_quarter + step, nq)
            for index in range(2):
                quarter_copy(index, frame, step, source, source).wait_recv()
                for hop in range(1, ns):
                    sent.append(
                        sub_copy(
                            index, frame, hop, step, lax.rem(my_sub + hop, ns), source, my_sub
                        )
                    )
                    sent[-1].start()

    def spatial_frame(frame):
        for quarter_step in range(nq):
            quarter = lax.rem(my_quarter + quarter_step, nq)
            for step in range(1, ns):
                source = lax.rem(my_sub + step, ns)
                for index in range(2):
                    sub_copy(
                        index, frame, step, quarter_step, source, quarter, source
                    ).wait_recv()
        o_sp[frame] = attend(q_sp[frame], k_sp[frame], v_sp[frame], score_scale)
        put = pltpu.make_async_copy(
            o_sp.at[frame], out.at[frame, :, first], local_sem.at[6 + frame]
        )
        put.start()
        return put

    def temporal_chunk(chunk):
        for place in range(n - 1):
            source = peer_at(place)
            for index in range(3):
                strip_copy(index, chunk, place, source, source).wait_recv()
        for lower in range(chunk * rows_chunk, (chunk + 1) * rows_chunk, STRIP):
            strip = [
                buffer[:, lower : lower + STRIP, :].reshape(n * frames * STRIP, width)
                for buffer in temporal_buf
            ]
            mixed = attend(*strip, score_scale)
            o_tm[:, lower : lower + STRIP, :] = mixed.reshape(n * frames, STRIP, width)
        for place in range(n - 1):
            sent.append(return_copy(chunk, place, peer_at(place), me))
            sent[-1].start()
        lower = pl.multiple_of(me * rows + chunk * rows_chunk, STRIP)
        put = pltpu.make_async_copy(
            o_tm.at[my_frames, pl.ds(chunk * rows_chunk, rows_chunk), :],
            out.at[:, pl.ds(lower, rows_chunk), second],
            local_sem.at[6 + frames + chunk],
        )
        put.start()
        return put

    puts = []
    forward(0)
    puts.append(spatial_frame(0))
    for frame in range(1, frames):
        forward(frame)
    puts.append(temporal_chunk(0))
    for frame in range(1, frames):
        puts.append(spatial_frame(frame))
    for chunk in range(1, chunks):
        puts.append(temporal_chunk(chunk))
    for chunk in range(chunks):
        for place in range(n - 1):
            source = peer_at(place)
            return_copy(chunk, place, source, source).wait_recv()
    for put in puts:
        put.wait()
    for copy in sent:
        copy.wait_send()


def body(mesh, queries, keys, values):
    frames, tokens, both = queries.shape
    width = both // 2
    n, nq, ns = mesh.shape["frame"], mesh.shape["quarter"], mesh.shape["sub"]
    chunks = math.gcd(tokens // (STRIP * n), 2)
    rows = tokens // n
    bf16 = jnp.bfloat16
    dma = pltpu.SemaphoreType.DMA
    spatial = pltpu.VMEM((frames, nq * ns * tokens, width), bf16)
    temporal = pltpu.VMEM((n * frames, rows, width), bf16)
    own = pltpu.VMEM((frames, tokens, width), bf16)
    return pl.pallas_call(
        functools.partial(kernel, (n, nq, ns, frames, tokens, width, chunks)),
        out_shape=jax.ShapeDtypeStruct(queries.shape, bf16),
        in_specs=[pl.BlockSpec(memory_space=pl.ANY)] * 3,
        out_specs=pl.BlockSpec(memory_space=pl.ANY),
        scratch_shapes=[
            own, spatial, spatial, temporal, temporal, temporal, temporal, own,
            dma((6 + frames + chunks,)),
            dma((3 * chunks * n,)), dma((3 * chunks * n,)),
            dma((chunks * n,)), dma((chunks * n,)),
            dma((2 * frames * nq,)), dma((2 * frames * nq,)),
            dma((2 * frames * nq * ns,)), dma((2 * frames * nq * ns,)),
        ],
        compiler_params=pltpu.CompilerParams(collective_id=0, has_side_effects=True),
    )(queries, keys, values)


def solution(mesh):
    spec = P(("groups", "frame"), ("quarter", "sub"), None)
    return jax.shard_map(
        functools.partial(body, mesh),
        mesh=mesh,
        in_specs=(spec, spec, spec),
        out_specs=spec,
        check_vma=False,
    )
```

```python
import functools
import math

import jax
import jax.numpy as jnp
from jax import lax
from jax.experimental import pallas as pl
from jax.experimental.pallas import tpu as pltpu
from jax.sharding import PartitionSpec as P

STRIP = 16
MESH = pl.DeviceIdType.MESH


def attend(query_rows, key_rows, value_rows, score_scale):
    scores = lax.dot_general(
        query_rows, key_rows, (((1,), (1,)), ((), ())), preferred_element_type=jnp.float32
    )
    highest = jnp.max(scores, axis=-1, keepdims=True)
    expo = jnp.exp((scores - highest) * score_scale)
    totals = jnp.sum(expo, axis=-1, keepdims=True)
    mixed = jnp.dot(expo.astype(jnp.bfloat16), value_rows, preferred_element_type=jnp.float32)
    return (mixed / totals).astype(jnp.bfloat16)


def kernel(
    sizes,
    q_in, k_in, v_in, out,
    q_sp, k_sp, v_sp, q_tm, k_tm, v_tm, o_tm, o_sp,
    local_sem, z_send, z_recv, r_send, r_recv, x_send, x_recv, s_send, s_recv,
):
    n, nq, ns, frames, tokens, width, chunks = sizes
    rows = tokens // n
    rows_chunk = rows // chunks
    score_scale = 1.0 / math.sqrt(width)
    me = lax.axis_index("frame")
    my_quarter = lax.axis_index("quarter")
    my_sub = lax.axis_index("sub")
    temporal_in = (q_in, k_in, v_in)
    temporal_buf = (q_tm, k_tm, v_tm)
    spatial_in = (k_in, v_in)
    spatial_buf = (k_sp, v_sp)
    first = slice(0, width)
    second = slice(width, 2 * width)

    barrier = pltpu.get_barrier_semaphore()
    for step in range(1, n):
        pl.semaphore_signal(
            barrier, inc=1, device_id={"frame": lax.rem(me + step, n)}, device_id_type=MESH
        )
    for step in range(1, nq):
        pl.semaphore_signal(
            barrier, inc=1, device_id={"quarter": lax.rem(my_quarter + step, nq)}, device_id_type=MESH
        )
    for step in range(1, ns):
        pl.semaphore_signal(
            barrier, inc=1, device_id={"sub": lax.rem(my_sub + step, ns)}, device_id_type=MESH
        )

    my_slot = my_quarter * ns + my_sub
    my_rows = pl.ds(pl.multiple_of(me * rows, STRIP), rows)
    my_tokens = pl.ds(pl.multiple_of(my_slot * tokens, tokens), tokens)
    my_frames = pl.ds(me * frames, frames)
    loads = [pltpu.make_async_copy(q_in.at[:, :, first], q_sp, local_sem.at[0])]
    for index in range(2):
        loads.append(
            pltpu.make_async_copy(
                spatial_in[index].at[:, :, first],
                spatial_buf[index].at[:, my_tokens, :],
                local_sem.at[1 + index],
            )
        )
    for index in range(3):
        loads.append(
            pltpu.make_async_copy(
                temporal_in[index].at[:, my_rows, second],
                temporal_buf[index].at[my_frames],
                local_sem.at[3 + index],
            )
        )
    for load in loads:
        load.start()

    pl.semaphore_wait(barrier, (n - 1) + (nq - 1) + (ns - 1))

    low = (me < n // 2).astype(jnp.int32)

    def peer_at(place):
        down = n - 1 - place
        down = down - (down <= me).astype(jnp.int32)
        up = place + (place >= me).astype(jnp.int32)
        return low * down + (1 - low) * up

    def strip_copy(index, chunk, place, target, source):
        lower = pl.multiple_of(target * rows + chunk * rows_chunk, STRIP)
        return pltpu.make_async_remote_copy(
            src_ref=temporal_in[index].at[:, pl.ds(lower, rows_chunk), second],
            dst_ref=temporal_buf[index].at[
                pl.ds(source * frames, frames), pl.ds(chunk * rows_chunk, rows_chunk), :
            ],
            send_sem=z_send.at[(index * chunks + chunk) * n + place],
            recv_sem=z_recv.at[(index * chunks + chunk) * n + source],
            device_id={"frame": target},
            device_id_type=MESH,
        )

    def return_copy(chunk, place, target, source):
        lower = pl.multiple_of(source * rows + chunk * rows_chunk, STRIP)
        return pltpu.make_async_remote_copy(
            src_ref=o_tm.at[
                pl.ds(target * frames, frames), pl.ds(chunk * rows_chunk, rows_chunk), :
            ],
            dst_ref=out.at[:, pl.ds(lower, rows_chunk), second],
            send_sem=r_send.at[chunk * n + place],
            recv_sem=r_recv.at[chunk * n + source],
            device_id={"frame": target},
            device_id_type=MESH,
        )

    def quarter_copy(index, frame, step, target, source):
        place = pl.ds(pl.multiple_of((source * ns + my_sub) * tokens, tokens), tokens)
        return pltpu.make_async_remote_copy(
            src_ref=spatial_in[index].at[frame, :, first],
            dst_ref=spatial_buf[index].at[frame, place, :],
            send_sem=x_send.at[(index * frames + frame) * nq + step],
            recv_sem=x_recv.at[(index * frames + frame) * nq + source],
            device_id={"quarter": target},
            device_id_type=MESH,
        )

    def sub_copy(index, frame, step, quarter_step, target, quarter, source):
        place = pl.ds(pl.multiple_of((quarter * ns + source) * tokens, tokens), tokens)
        landed = spatial_buf[index].at[frame, place, :]
        return pltpu.make_async_remote_copy(
            src_ref=spatial_in[index].at[frame, :, first] if quarter_step == 0 else landed,
            dst_ref=landed,
            send_sem=s_send.at[((index * frames + frame) * nq + quarter_step) * ns + step],
            recv_sem=s_recv.at[((index * frames + frame) * nq + quarter) * ns + source],
            device_id={"sub": target},
            device_id_type=MESH,
        )

    sent = []
    for chunk in range(chunks):
        for place in range(n - 1):
            for index in range(3):
                sent.append(strip_copy(index, chunk, place, peer_at(place), me))
                sent[-1].start()
        if chunk == 0:
            for frame in range(frames):
                for index in range(2):
                    for step in range(1, nq):
                        sent.append(
                            quarter_copy(
                                index, frame, step, lax.rem(my_quarter + step, nq), my_quarter
                            )
                        )
                        sent[-1].start()
                    for step in range(1, ns):
                        sent.append(
                            sub_copy(
                                index, frame, step, 0, lax.rem(my_sub + step, ns), my_quarter, my_sub
                            )
                        )
                        sent[-1].start()
    for load in loads:
        load.wait()

    def forward(frame):
        for step in range(1, nq):
            source = lax.rem(my_quarter + step, nq)
            for index in range(2):
                quarter_copy(index, frame, step, source, source).wait_recv()
                for hop in range(1, ns):
                    sent.append(
                        sub_copy(
                            index, frame, hop, step, lax.rem(my_sub + hop, ns), source, my_sub
                        )
                    )
                    sent[-1].start()

    def spatial_frame(frame):
        for quarter_step in range(nq):
            quarter = lax.rem(my_quarter + quarter_step, nq)
            for step in range(1, ns):
                source = lax.rem(my_sub + step, ns)
                for index in range(2):
                    sub_copy(
                        index, frame, step, quarter_step, source, quarter, source
                    ).wait_recv()
        o_sp[frame] = attend(q_sp[frame], k_sp[frame], v_sp[frame], score_scale)
        put = pltpu.make_async_copy(
            o_sp.at[frame], out.at[frame, :, first], local_sem.at[6 + frame]
        )
        put.start()
        return put

    def temporal_chunk(chunk):
        for place in range(n - 1):
            source = peer_at(place)
            for index in range(3):
                strip_copy(index, chunk, place, source, source).wait_recv()
        for lower in range(chunk * rows_chunk, (chunk + 1) * rows_chunk, STRIP):
            strip = [
                buffer[:, lower : lower + STRIP, :].reshape(n * frames * STRIP, width)
                for buffer in temporal_buf
            ]
            mixed = attend(*strip, score_scale)
            o_tm[:, lower : lower + STRIP, :] = mixed.reshape(n * frames, STRIP, width)
        for place in range(n - 1):
            sent.append(return_copy(chunk, place, peer_at(place), me))
            sent[-1].start()
        lower = pl.multiple_of(me * rows + chunk * rows_chunk, STRIP)
        put = pltpu.make_async_copy(
            o_tm.at[my_frames, pl.ds(chunk * rows_chunk, rows_chunk), :],
            out.at[:, pl.ds(lower, rows_chunk), second],
            local_sem.at[6 + frames + chunk],
        )
        put.start()
        return put

    puts = []
    forward(0)
    puts.append(spatial_frame(0))
    for frame in range(1, frames):
        forward(frame)
    puts.append(temporal_chunk(0))
    for frame in range(1, frames):
        puts.append(spatial_frame(frame))
    for chunk in range(1, chunks):
        puts.append(temporal_chunk(chunk))
    for chunk in range(chunks):
        for place in range(n - 1):
            source = peer_at(place)
            return_copy(chunk, place, source, source).wait_recv()
    for put in puts:
        put.wait()
    for copy in sent:
        copy.wait_send()


def body(mesh, queries, keys, values):
    frames, tokens, both = queries.shape
    width = both // 2
    n, nq, ns = mesh.shape["frame"], mesh.shape["quarter"], mesh.shape["sub"]
    chunks = math.gcd(tokens // (STRIP * n), 2)
    rows = tokens // n
    bf16 = jnp.bfloat16
    dma = pltpu.SemaphoreType.DMA
    spatial = pltpu.VMEM((frames, nq * ns * tokens, width), bf16)
    temporal = pltpu.VMEM((n * frames, rows, width), bf16)
    own = pltpu.VMEM((frames, tokens, width), bf16)
    return pl.pallas_call(
        functools.partial(kernel, (n, nq, ns, frames, tokens, width, chunks)),
        out_shape=jax.ShapeDtypeStruct(queries.shape, bf16),
        in_specs=[pl.BlockSpec(memory_space=pltpu.HBM)] * 3,
        out_specs=pl.BlockSpec(memory_space=pl.ANY),
        scratch_shapes=[
            own, spatial, spatial, temporal, temporal, temporal, temporal, own,
            dma((6 + frames + chunks,)),
            dma((3 * chunks * n,)), dma((3 * chunks * n,)),
            dma((chunks * n,)), dma((chunks * n,)),
            dma((2 * frames * nq,)), dma((2 * frames * nq,)),
            dma((2 * frames * nq * ns,)), dma((2 * frames * nq * ns,)),
        ],
        compiler_params=pltpu.CompilerParams(collective_id=0, has_side_effects=True, vmem_limit_bytes=24 << 20),
    )(*[pltpu.with_memory_space_constraint(a, pltpu.HBM) for a in (queries, keys, values)])


def solution(mesh):
    spec = P(("groups", "frame"), ("quarter", "sub"), None)
    return jax.shard_map(
        functools.partial(body, mesh),
        mesh=mesh,
        in_specs=(spec, spec, spec),
        out_specs=spec,
        check_vma=False,
    )
```

```python
import functools
import math

import jax
import jax.numpy as jnp
from jax import lax
from jax.experimental import pallas as pl
from jax.experimental.pallas import tpu as pltpu
from jax.sharding import PartitionSpec as P

STRIP = 16
MESH = pl.DeviceIdType.MESH


def attend(query_rows, key_rows, value_rows, score_scale):
    scores = lax.dot_general(
        query_rows, key_rows, (((1,), (1,)), ((), ())), preferred_element_type=jnp.float32
    )
    highest = jnp.max(scores, axis=-1, keepdims=True)
    expo = jnp.exp((scores - highest) * score_scale)
    totals = jnp.sum(expo, axis=-1, keepdims=True)
    mixed = jnp.dot(expo.astype(jnp.bfloat16), value_rows, preferred_element_type=jnp.float32)
    return (mixed / totals).astype(jnp.bfloat16)


def kernel(
    sizes,
    q_in, k_in, v_in, out,
    q_sp, k_sp, v_sp, q_tm, k_tm, v_tm, o_tm, o_sp,
    local_sem, z_send, z_recv, r_send, r_recv, x_send, x_recv, s_send, s_recv,
):
    n, nq, ns, frames, tokens, width, chunks = sizes
    rows = tokens // n
    rows_chunk = rows // chunks
    score_scale = 1.0 / math.sqrt(width)
    me = lax.axis_index("frame")
    my_quarter = lax.axis_index("quarter")
    my_sub = lax.axis_index("sub")
    temporal_in = (q_in, k_in, v_in)
    temporal_buf = (q_tm, k_tm, v_tm)
    spatial_in = (k_in, v_in)
    spatial_buf = (k_sp, v_sp)
    first = slice(0, width)
    second = slice(width, 2 * width)

    barrier = pltpu.get_barrier_semaphore()
    for step in range(1, n):
        pl.semaphore_signal(
            barrier, inc=1, device_id={"frame": lax.rem(me + step, n)}, device_id_type=MESH
        )
    for step in range(1, nq):
        pl.semaphore_signal(
            barrier, inc=1, device_id={"quarter": lax.rem(my_quarter + step, nq)}, device_id_type=MESH
        )
    for step in range(1, ns):
        pl.semaphore_signal(
            barrier, inc=1, device_id={"sub": lax.rem(my_sub + step, ns)}, device_id_type=MESH
        )

    my_slot = my_quarter * ns + my_sub
    my_rows = pl.ds(pl.multiple_of(me * rows, STRIP), rows)
    my_tokens = pl.ds(pl.multiple_of(my_slot * tokens, tokens), tokens)
    my_frames = pl.ds(me * frames, frames)
    loads = [pltpu.make_async_copy(q_in.at[:, :, first], q_sp, local_sem.at[0])]
    for index in range(2):
        loads.append(
            pltpu.make_async_copy(
                spatial_in[index].at[:, :, first],
                spatial_buf[index].at[:, my_tokens, :],
                local_sem.at[1 + index],
            )
        )
    for index in range(3):
        loads.append(
            pltpu.make_async_copy(
                temporal_in[index].at[:, my_rows, second],
                temporal_buf[index].at[my_frames],
                local_sem.at[3 + index],
            )
        )
    for load in loads:
        load.start()

    pl.semaphore_wait(barrier, (n - 1) + (nq - 1) + (ns - 1))

    low = (me < n // 2).astype(jnp.int32)

    def peer_at(place):
        down = n - 1 - place
        down = down - (down <= me).astype(jnp.int32)
        up = place + (place >= me).astype(jnp.int32)
        return low * down + (1 - low) * up

    def strip_copy(index, chunk, place, target, source):
        lower = pl.multiple_of(target * rows + chunk * rows_chunk, STRIP)
        return pltpu.make_async_remote_copy(
            src_ref=temporal_in[index].at[:, pl.ds(lower, rows_chunk), second],
            dst_ref=temporal_buf[index].at[
                pl.ds(source * frames, frames), pl.ds(chunk * rows_chunk, rows_chunk), :
            ],
            send_sem=z_send.at[(index * chunks + chunk) * n + place],
            recv_sem=z_recv.at[(index * chunks + chunk) * n + source],
            device_id={"frame": target},
            device_id_type=MESH,
        )

    def return_copy(chunk, place, target, source):
        lower = pl.multiple_of(source * rows + chunk * rows_chunk, STRIP)
        return pltpu.make_async_remote_copy(
            src_ref=o_tm.at[
                pl.ds(target * frames, frames), pl.ds(chunk * rows_chunk, rows_chunk), :
            ],
            dst_ref=out.at[:, pl.ds(lower, rows_chunk), second],
            send_sem=r_send.at[chunk * n + place],
            recv_sem=r_recv.at[chunk * n + source],
            device_id={"frame": target},
            device_id_type=MESH,
        )

    def quarter_copy(index, frame, step, target, source):
        place = pl.ds(pl.multiple_of((source * ns + my_sub) * tokens, tokens), tokens)
        return pltpu.make_async_remote_copy(
            src_ref=spatial_in[index].at[frame, :, first],
            dst_ref=spatial_buf[index].at[frame, place, :],
            send_sem=x_send.at[(index * frames + frame) * nq + step],
            recv_sem=x_recv.at[(index * frames + frame) * nq + source],
            device_id={"quarter": target},
            device_id_type=MESH,
        )

    def sub_copy(index, frame, step, quarter_step, target, quarter, source):
        place = pl.ds(pl.multiple_of((quarter * ns + source) * tokens, tokens), tokens)
        landed = spatial_buf[index].at[frame, place, :]
        return pltpu.make_async_remote_copy(
            src_ref=spatial_in[index].at[frame, :, first] if quarter_step == 0 else landed,
            dst_ref=landed,
            send_sem=s_send.at[((index * frames + frame) * nq + quarter_step) * ns + step],
            recv_sem=s_recv.at[((index * frames + frame) * nq + quarter) * ns + source],
            device_id={"sub": target},
            device_id_type=MESH,
        )

    sent = []
    for place in range(n - 1):
        for chunk in range(chunks):
            for index in range(3):
                sent.append(strip_copy(index, chunk, place, peer_at(place), me))
                sent[-1].start()
    for frame in range(frames):
        for index in range(2):
            for step in range(1, nq):
                sent.append(
                    quarter_copy(index, frame, step, lax.rem(my_quarter + step, nq), my_quarter)
                )
                sent[-1].start()
            for step in range(1, ns):
                sent.append(
                    sub_copy(
                        index, frame, step, 0, lax.rem(my_sub + step, ns), my_quarter, my_sub
                    )
                )
                sent[-1].start()
    for load in loads:
        load.wait()

    def forward(frame):
        for step in range(1, nq):
            source = lax.rem(my_quarter + step, nq)
            for index in range(2):
                quarter_copy(index, frame, step, source, source).wait_recv()
                for hop in range(1, ns):
                    sent.append(
                        sub_copy(
                            index, frame, hop, step, lax.rem(my_sub + hop, ns), source, my_sub
                        )
                    )
                    sent[-1].start()

    def spatial_frame(frame):
        for quarter_step in range(nq):
            quarter = lax.rem(my_quarter + quarter_step, nq)
            for step in range(1, ns):
                source = lax.rem(my_sub + step, ns)
                for index in range(2):
                    sub_copy(
                        index, frame, step, quarter_step, source, quarter, source
                    ).wait_recv()
        o_sp[frame] = attend(q_sp[frame], k_sp[frame], v_sp[frame], score_scale)
        put = pltpu.make_async_copy(
            o_sp.at[frame], out.at[frame, :, first], local_sem.at[6 + frame]
        )
        put.start()
        return put

    def temporal_chunk(chunk):
        for place in range(n - 1):
            source = peer_at(place)
            for index in range(3):
                strip_copy(index, chunk, place, source, source).wait_recv()
        for lower in range(chunk * rows_chunk, (chunk + 1) * rows_chunk, STRIP):
            strip = [
                buffer[:, lower : lower + STRIP, :].reshape(n * frames * STRIP, width)
                for buffer in temporal_buf
            ]
            mixed = attend(*strip, score_scale)
            o_tm[:, lower : lower + STRIP, :] = mixed.reshape(n * frames, STRIP, width)
        for place in range(n - 1):
            sent.append(return_copy(chunk, place, peer_at(place), me))
            sent[-1].start()
        lower = pl.multiple_of(me * rows + chunk * rows_chunk, STRIP)
        put = pltpu.make_async_copy(
            o_tm.at[my_frames, pl.ds(chunk * rows_chunk, rows_chunk), :],
            out.at[:, pl.ds(lower, rows_chunk), second],
            local_sem.at[6 + frames + chunk],
        )
        put.start()
        return put

    puts = []
    forward(0)
    puts.append(spatial_frame(0))
    for frame in range(1, frames):
        forward(frame)
    puts.append(temporal_chunk(0))
    for chunk in range(1, chunks):
        puts.append(temporal_chunk(chunk))
    for frame in range(1, frames):
        puts.append(spatial_frame(frame))
    for chunk in range(chunks):
        for place in range(n - 1):
            source = peer_at(place)
            return_copy(chunk, place, source, source).wait_recv()
    for put in puts:
        put.wait()
    for copy in sent:
        copy.wait_send()


def body(mesh, queries, keys, values):
    frames, tokens, both = queries.shape
    width = both // 2
    n, nq, ns = mesh.shape["frame"], mesh.shape["quarter"], mesh.shape["sub"]
    chunks = math.gcd(tokens // (STRIP * n), 2)
    rows = tokens // n
    bf16 = jnp.bfloat16
    dma = pltpu.SemaphoreType.DMA
    spatial = pltpu.VMEM((frames, nq * ns * tokens, width), bf16)
    temporal = pltpu.VMEM((n * frames, rows, width), bf16)
    own = pltpu.VMEM((frames, tokens, width), bf16)
    return pl.pallas_call(
        functools.partial(kernel, (n, nq, ns, frames, tokens, width, chunks)),
        out_shape=jax.ShapeDtypeStruct(queries.shape, bf16),
        in_specs=[pl.BlockSpec(memory_space=pltpu.HBM)] * 3,
        out_specs=pl.BlockSpec(memory_space=pl.ANY),
        scratch_shapes=[
            own, spatial, spatial, temporal, temporal, temporal, temporal, own,
            dma((6 + frames + chunks,)),
            dma((3 * chunks * n,)), dma((3 * chunks * n,)),
            dma((chunks * n,)), dma((chunks * n,)),
            dma((2 * frames * nq,)), dma((2 * frames * nq,)),
            dma((2 * frames * nq * ns,)), dma((2 * frames * nq * ns,)),
        ],
        compiler_params=pltpu.CompilerParams(collective_id=0, has_side_effects=True, vmem_limit_bytes=24 << 20),
    )(*[pltpu.with_memory_space_constraint(a, pltpu.HBM) for a in (queries, keys, values)])


def solution(mesh):
    spec = P(("groups", "frame"), ("quarter", "sub"), None)
    return jax.shard_map(
        functools.partial(body, mesh),
        mesh=mesh,
        in_specs=(spec, spec, spec),
        out_specs=spec,
        check_vma=False,
    )
```
